32 devices in a mesh: row: 4 (over y, x), col: 8 (over z, core).
Axes of the slice: x: 2, y: 2, z: 4, core: 2. Of those that a mesh axis runs over, the one named last changes fastest.
Arguments:
- ainv: float32 [24576, 24576], P('row', 'col'), may hold values from -0.0390625 to 0.0390625
- lpanel: float32 [24576, 1024], P(('row', 'col')), may hold values from -0.6 to 0.6
- dinv: float32 [1024, 512], P(('row', 'col')), may hold values from -6 to 6
- lmask: int32 [384, 2], P(('row', 'col')), may hold values 0 or 1
- hrows: float32 [24576, 1024], P(('row', 'col')), may hold values from -6 to 6
- hmask: int32 [384, 2], P(('row', 'col')), may hold values 0 or 1
- pole_weight: float32 [1], replicated, may hold values from 0.5 to 2
Outputs:
- offdiag: float32 [24576, 1024], P(('row', 'col'))
- diaginv: float32 [1024, 512], P(('row', 'col'))
- energy: float32 [24576], P(('row', 'col'))
The draws below stay inside these ranges and needn't reach their ends.
All inputs are finite; a program needn't handle non-finite values. No bound on the sum of `lmask` or of `hmask` on one device may be relied on, other than what follows from the above.
Results may differ from the reference program's by a relative error of at most 0.00024.
Values sent between devices are 32-bit elements; how exact they have to be, the bound alone decides.
A program may use at most 192 MiB of HBM per device.

```python
import jax
import jax.numpy as jnp
from jax import lax

NC = 24576
SN = 512
BLK = 64
W = 1024
NB = 384


def plant(values, key, low, largest):
    index_at = [jax.random.randint(jax.random.fold_in(key, axis), (), 0, length) for axis, length in enumerate(values.shape)]
    longest = values.shape.index(max(values.shape))
    beside = index_at[:longest] + [(index_at[longest] + 1) % values.shape[longest]] + index_at[longest + 1:]
    return values.at[tuple(index_at)].set(low).at[tuple(beside)].set(largest)


def steps_of(rng, shape, split, least, high):
    factor_of = 1.0
    for axis_at, parts in split:
        steps = jax.random.uniform(jax.random.fold_in(jax.random.fold_in(rng, 6), axis_at), (parts,), jnp.float32, least / len(split), high / len(split))
        factor_of = factor_of * jnp.repeat(jnp.exp(steps), shape[axis_at] // parts).reshape((-1,) + (1,) * (len(shape) - 1 - axis_at))
    return factor_of


def gaussian(own_key, dims, spread, limit, shards=(), held_as=jnp.bfloat16):
    array = jax.random.normal(own_key, dims, jnp.float32) * spread
    if len(shards) > 0:
        array = steps_of(own_key, dims, shards, -0.22, 0.18) * array
    return jnp.clip(array, min=-limit, max=limit).astype(held_as)


def setup_inputs(seed: int = 0) -> dict:
    streams_of = jax.random.split(jax.random.key(seed), 8)
    ainv = gaussian(streams_of[0], (NC, NC), NC ** -0.5, 0.0390625, ((0, 4), (1, 8)), jnp.float32)
    lpanel = gaussian(streams_of[1], (NC, W), 0.08, 0.6, ((0, 32),), jnp.float32)
    dinv = gaussian(streams_of[2], (W, SN), 1.0, 6.0, ((0, 32),), jnp.float32)
    lmask = plant((jax.random.randint(streams_of[3], (NB, 2), 0, 2) < 1).astype(jnp.int32), jax.random.fold_in(streams_of[3], 1), 0, 1)
    hrows = gaussian(streams_of[4], (NC, W), 1.0, 6.0, ((0, 32),), jnp.float32)
    hmask = plant((jax.random.randint(streams_of[5], (NB, 2), 0, 3) < 2).astype(jnp.int32), jax.random.fold_in(streams_of[5], 1), 0, 1)
    pole_weight = jnp.clip(jax.random.uniform(streams_of[6], (1,), jnp.float32, 0.5, 2.0), 0.5, 2.0)
    return {"ainv": ainv, "lpanel": lpanel, "dinv": dinv, "lmask": lmask, "hrows": hrows, "hmask": hmask, "pole_weight": pole_weight}


def expand_mask(mask):
    full = jnp.broadcast_to(mask.astype(jnp.float32)[:, None, :, None], (NB, BLK, 2, SN))
    return full.reshape(NC, W)


def reference(ainv, lpanel, dinv, lmask, hrows, hmask, pole_weight):
    pattern = expand_mask(lmask)
    lmasked = lpanel * pattern
    ycol = jnp.dot(ainv, lmasked, precision=lax.Precision.HIGHEST, preferred_element_type=jnp.float32)
    offdiag = -ycol * pattern
    left = lmasked.reshape(NC, 2, SN)
    right = ycol.reshape(NC, 2, SN)
    blocks = jnp.einsum("rsa,rsb->sab", left, right, precision=lax.Precision.HIGHEST)
    diaginv = dinv + blocks.reshape(W, SN)
    hpattern = expand_mask(hmask)
    energy = pole_weight[0] * jnp.sum(hrows * hpattern * offdiag, axis=1)
    return offdiag, diaginv, energy
```

```python
import jax
import jax.numpy as jnp
from jax import lax
from jax.sharding import PartitionSpec as P


def expand_local(mask, block_rows, columns):
    count = mask.shape[0]
    full = jnp.broadcast_to(
        mask.astype(jnp.float32)[:, None, None], (count, block_rows, columns)
    )
    return full.reshape(count * block_rows, columns)


def to_grid_column(block):
    rows, cols = lax.axis_size("row"), lax.axis_size("col")
    pairs = [(g, (g % rows) * cols + g // rows) for g in range(rows * cols)]
    return lax.ppermute(block, ("row", "col"), pairs)


def local(ainv, lpanel, dinv, lmask, hrows, hmask, pole_weight):
    rows_local = lpanel.shape[0]
    supernode = lpanel.shape[1] // 2
    block_rows = rows_local // lmask.shape[0]
    rows, cols = lax.axis_size("row"), lax.axis_size("col")
    owned_diag = dinv.shape[0]
    offdiags, diags, energy = [], [], 0.0
    for s in range(2):
        at = slice(s * supernode, (s + 1) * supernode)
        pattern = expand_local(lmask[:, s], block_rows, supernode)
        lmasked = lpanel[:, at] * pattern
        colpanel = lax.all_gather(to_grid_column(lmasked), "row", axis=0, tiled=True)
        partial_value = jnp.dot(
            ainv, colpanel, precision=lax.Precision.HIGH, preferred_element_type=jnp.float32
        )
        owned = lax.psum_scatter(partial_value, "col", scatter_dimension=0, tiled=True)
        term = lax.dot_general(
            lmasked, owned, (((0,), (0,)), ((), ())), precision=lax.Precision.HIGH,
            preferred_element_type=jnp.float32,
        )
        half = supernode // (cols * owned_diag)
        term = term.reshape(half, cols, owned_diag, supernode).transpose(1, 0, 2, 3)
        diags.append(lax.psum_scatter(term, "col", scatter_dimension=0, tiled=False))
        offdiag = -owned * pattern
        offdiags.append(offdiag)
        hpattern = expand_local(hmask[:, s], block_rows, supernode)
        energy = energy + jnp.sum(hrows[:, at] * hpattern * offdiag, axis=1)
    diag = jnp.concatenate(diags, axis=0)
    diag_sum = lax.psum_scatter(diag, "row", scatter_dimension=0, tiled=False)
    return (jnp.concatenate(offdiags, axis=1), dinv + diag_sum, pole_weight[0] * energy)


def solution(mesh):
    in_specs = (
        P("row", "col"),
        P(("row", "col"), None),
        P(("row", "col"), None),
        P(("row", "col"), None),
        P(("row", "col"), None),
        P(("row", "col"), None),
        P(),
    )
    out_specs = (P(("row", "col"), None), P(("row", "col"), None), P(("row", "col")))
    return jax.shard_map(local, mesh=mesh, in_specs=in_specs, out_specs=out_specs, check_vma=False)
```

```python
import jax
import jax.numpy as jnp
from jax import lax
from jax.sharding import PartitionSpec as P

HALVES = 2


def expand_local(mask, block_rows, columns):
    count = mask.shape[0]
    full = jnp.broadcast_to(
        mask.astype(jnp.float32)[:, None, None], (count, block_rows, columns)
    )
    return full.reshape(count * block_rows, columns)


def meet(row, column):
    rows = lax.axis_size("row")
    return row ^ (column % rows)


def spread(block):
    rows, cols = lax.axis_size("row"), lax.axis_size("col")
    pairs = [(r * cols + c, meet(r, c) * cols + c) for r in range(rows) for c in range(cols)]
    return lax.ppermute(block, ("row", "col"), pairs)


def along(block):
    rows, cols = lax.axis_size("row"), lax.axis_size("col")
    pairs = [
        (meet(r, c) * cols + c, meet(r, c) * cols + r * (cols // rows) + c // rows)
        for r in range(rows) for c in range(cols)
    ]
    return lax.ppermute(block, ("row", "col"), pairs)


def gather(block):
    rows = lax.axis_size("row")
    return [block] + [
        lax.ppermute(block, "row", [(r, meet(r, d)) for r in range(rows)]) for d in range(1, rows)
    ]


def panel_of(held):
    rows, cols = lax.axis_size("row"), lax.axis_size("col")
    me, owner = lax.axis_index("row"), lax.axis_index("col") // (cols // rows)
    stacked = jnp.stack(held)
    order = [meet(me, meet(owner, k)) for k in range(rows)]
    return jnp.concatenate([lax.dynamic_index_in_dim(stacked, d, 0, False) for d in order])


def reduce_rows(term, axis):
    return jnp.sum(lax.all_to_all(term, axis, 0, 0), axis=0)


def local(ainv, lpanel, dinv, lmask, hrows, hmask, pole_weight):
    rows_local = lpanel.shape[0]
    supernode = lpanel.shape[1] // 2
    width = supernode // HALVES
    block_rows = rows_local // lmask.shape[0]
    rows, cols = lax.axis_size("row"), lax.axis_size("col")
    patterns = [expand_local(lmask[:, s], block_rows, supernode) for s in range(2)]
    lmasked = [lpanel[:, s * supernode:(s + 1) * supernode] * patterns[s] for s in range(2)]

    order = [(s, h) for h in range(HALVES) for s in range(2)]
    blocks = [lmasked[s][:, h * width:(h + 1) * width] for s, h in order]
    count = len(order)
    state = {("block", j): block for j, block in enumerate(blocks)}
    for t in range(count + 3):
        done = {}
        if t < count:
            done["spread", t] = spread(state.pop(("block", t)))
        if 0 <= t - 1 < count:
            done["along", t - 1] = along(state.pop(("spread", t - 1)))
        if 0 <= t - 2 < count:
            done["held", t - 2] = gather(state.pop(("along", t - 2)))
        if 0 <= t - 3 < count:
            done["partial", t - 3] = jnp.dot(
                ainv, panel_of(state.pop(("held", t - 3))), precision=lax.Precision.HIGH,
                preferred_element_type=jnp.float32,
            )
        partials = {k: v for k, v in state.items() if k[0] == "partial"}
        rest = {k: v for k, v in state.items() if k[0] != "partial"} | done
        keys = list(rest)
        state = dict(zip(keys, lax.optimization_barrier([rest[k] for k in keys]))) | partials

    owned, terms, diags = {}, [], []
    for j, (s, h) in enumerate(order):
        y = lax.psum_scatter(state["partial", j], "col", scatter_dimension=0, tiled=True)
        owned[s, h] = y
        terms.append(lax.dot_general(
            lmasked[s], y, (((0,), (0,)), ((), ())), precision=lax.Precision.HIGH,
            preferred_element_type=jnp.float32,
        ))
        if s == 1:
            term = jnp.concatenate(terms, axis=0).reshape(rows, -1, width)
            term = reduce_rows(term, "row").reshape(cols, -1, width)
            diags.append(reduce_rows(term, "col"))
            terms = []
    ycol = jnp.concatenate([owned[s, h] for s in range(2) for h in range(HALVES)], axis=1)
    offdiag = -ycol * jnp.concatenate(patterns, axis=1)
    hpattern = jnp.concatenate([expand_local(hmask[:, s], block_rows, supernode) for s in range(2)], axis=1)
    energy = pole_weight[0] * jnp.sum(hrows * hpattern * offdiag, axis=1)
    return (offdiag, dinv + jnp.concatenate(diags, axis=1), energy)


def solution(mesh):
    in_specs = (
        P("row", "col"),
        P(("row", "col"), None),
        P(("row", "col"), None),
        P(("row", "col"), None),
        P(("row", "col"), None),
        P(("row", "col"), None),
        P(),
    )
    out_specs = (P(("row", "col"), None), P(("row", "col"), None), P(("row", "col")))
    return jax.shard_map(local, mesh=mesh, in_specs=in_specs, out_specs=out_specs, check_vma=False)
```
